128 devices in a mesh: req: 16 (over x, z), mlp: 8 (over y, core).
Axes of the slice: x: 4, y: 4, z: 4, core: 2. Of those that a mesh axis runs over, the one named last changes fastest.
Arguments:
- patches: bfloat16 [15360, 4096], P('req'), may hold values from -6 to 6
- norm_gain: float32 [4096], replicated, may hold values from 0.25 to 1.75
- norm_bias: float32 [4096], replicated, may hold values from -3 to 3
- gate_weight: bfloat16 [4096, 8192], P(None, ('req', 'mlp')), may hold values from -0.09375 to 0.09375
- up_weight: bfloat16 [4096, 8192], P(None, ('req', 'mlp')), may hold values from -0.09375 to 0.09375
- down_weight: bfloat16 [4096, 8192], P(None, ('req', 'mlp')), may hold values from -0.0625 to 0.0625
- layer_scale: float32 [4096], replicated, may hold values from 0.25 to 2.5
- projection: bfloat16 [4, 4096, 4096], P(None, 'mlp', 'req'), may hold values from -0.046875 to 0.046875
- text_rows: bfloat16 [65536, 4096], P(('req', 'mlp')), may hold values from -6 to 6
- destination: int32 [3840], replicated, may hold values from -1 to 65535, as said below
Outputs:
- patch_out: bfloat16 [15360, 4096], P('req', 'mlp')
- streams: bfloat16 [65536, 4096], P(('req', 'mlp'))
The draws below stay inside these ranges and needn't reach their ends.
Inputs may be any that keep to these rules, and one draw needn't show every extreme that they name: `destination`: values other than -1 are distinct positions; the positions landing in one piece of 512 consecutive positions (a stream holds 8 pieces) form one run of consecutive positions, at least one and at most 30 of them, and some piece receives exactly 30.
All inputs are finite; a program needn't handle non-finite values.
Results may differ from the reference program's by a relative error of at most 0.015.
Values may be sent and summed in bfloat16 or wider, within the bound.
No kernel may reach another device: no remote copies, remote signals or barrier semaphores. Data moves between devices by JAX's collectives and lax.ppermute only.
A program may use at most 128 MiB of HBM per device.

```python
import math
import jax
import jax.numpy as jnp
from jax import lax

D = 4096
FF = 8192
DOUT = 4096
L = 4096
PATCHES = 15360
SLOTS = 3840
NS = 16
PIECE = 512
CAP = 30
N_REQ = 16
N_MLP = 8


def draw_destination(key, part):
    cells = NS * N_MLP
    key_count, key_top, key_start, key_order = jax.random.split(jax.random.fold_in(key, 17), 4)
    counts = jax.random.randint(key_count, (cells,), (CAP + 1) // 2, CAP + 1)
    chosen = jax.random.randint(key_top, (), 0, cells)
    cell_ids = jnp.arange(cells)
    counts = jnp.where(cell_ids == (chosen + 1) % cells, (CAP + 1) // 2, counts)
    counts = jnp.where(cell_ids == chosen, CAP, counts)
    starts = jax.random.randint(key_start, (cells,), 0, PIECE - counts + 1)
    starts = jnp.where(cell_ids == cells - 1, PIECE - counts, starts)
    row_index = jnp.arange(cells * CAP)
    cell_of = row_index // CAP
    rank_of = row_index % CAP
    values = jnp.where(rank_of < counts[cell_of], cell_of * PIECE + starts[cell_of] + rank_of, -1)
    order = jax.random.permutation(key_order, cells * CAP)
    return jnp.zeros((cells * CAP,), jnp.int32).at[order].set(values.astype(jnp.int32))


def shard_levels(stream_key, shape, cuts, least, top_value):
    def one(position, blocks):
        heights = jax.random.uniform(jax.random.fold_in(jax.random.fold_in(stream_key, 6), position), (blocks,), jnp.float32, least / len(cuts), top_value / len(cuts))
        return jnp.repeat(jnp.exp(heights), shape[position] // blocks).reshape((-1,) + (1,) * (len(shape) - position - 1))

    loudness = one(*cuts[0])
    for cut in cuts[1:]:
        loudness = loudness * one(*cut)
    return loudness


def bell_draw(stream_key, dims, width, reach, shards=(), held_as=jnp.bfloat16):
    result = width * jax.random.normal(stream_key, dims, jnp.float32)
    if shards:
        result = result * shard_levels(stream_key, dims, shards, -0.22, 0.18)
    return jnp.clip(result, -reach, reach).astype(held_as)


def setup_inputs(seed: int = 0) -> dict:
    key_list = jax.random.split(jax.random.key(seed), 11)
    return {
        "patches": bell_draw(key_list[0], (PATCHES, D), 1.0, 6.0, ((0, 16),)),
        "norm_gain": jnp.clip(1.0 + 0.15 * jax.random.normal(key_list[1], (D,), jnp.float32), 0.25, 1.75),
        "norm_bias": bell_draw(key_list[2], (D,), 0.5, 3.0, (), jnp.float32),
        "gate_weight": bell_draw(key_list[3], (D, FF), D ** -0.5, 0.09375, ((1, 128),)),
        "up_weight": bell_draw(key_list[4], (D, FF), D ** -0.5, 0.09375, ((1, 128),)),
        "down_weight": bell_draw(key_list[5], (D, FF), FF ** -0.5, 0.0625, ((1, 128),)),
        "layer_scale": jnp.clip(jnp.exp(jax.random.uniform(key_list[6], (D,), jnp.float32, math.log(0.25), math.log(2.5))), 0.25, 2.5),
        "projection": bell_draw(key_list[7], (4, D, DOUT), (4 * D) ** -0.5, 0.046875, ((1, 8), (2, 16))),
        "text_rows": bell_draw(key_list[8], (NS * L, DOUT), 1.0, 6.0, ((0, 128),)),
        "destination": draw_destination(jax.random.fold_in(key_list[10], 71), 0),
    }


def layer_norm(values, norm_gain, norm_bias):
    row_mean = lax.optimization_barrier(jnp.mean(values, axis=-1, keepdims=True))
    centred = values - row_mean
    variance = lax.optimization_barrier(jnp.mean(centred * centred, axis=-1, keepdims=True))
    return centred * lax.rsqrt(variance + 1e-06) * norm_gain + norm_bias

def reference(patches, norm_gain, norm_bias, gate_weight, up_weight, down_weight, layer_scale, projection, text_rows, destination):
    model_width = patches.shape[1]
    unit_block = FF // (N_REQ * N_MLP)
    inputs = patches.astype(jnp.float32)
    normed = layer_norm(inputs, norm_gain, norm_bias).astype(jnp.bfloat16)
    gate_grouped = gate_weight.reshape(model_width, N_REQ, N_MLP, unit_block)
    up_grouped = up_weight.reshape(model_width, N_REQ, N_MLP, unit_block)
    down_grouped = down_weight.reshape(model_width, N_REQ, N_MLP, unit_block)
    ffn_total = jnp.zeros(inputs.shape, jnp.float32)
    for group_index in range(N_MLP):
        gate_cols = gate_grouped[:, :, group_index, :].reshape(model_width, N_REQ * unit_block)
        up_cols = up_grouped[:, :, group_index, :].reshape(model_width, N_REQ * unit_block)
        down_cols = down_grouped[:, :, group_index, :].reshape(model_width, N_REQ * unit_block)
        gate_act = jnp.dot(normed, gate_cols, preferred_element_type=jnp.float32)
        up_act = jnp.dot(normed, up_cols, preferred_element_type=jnp.float32)
        hidden = (jax.nn.silu(gate_act) * up_act).astype(jnp.bfloat16)
        partial_value = jnp.dot(hidden, down_cols.T, preferred_element_type=jnp.float32).astype(jnp.bfloat16)
        ffn_total = ffn_total + lax.optimization_barrier(partial_value).astype(jnp.float32)
    patch_out = (inputs + layer_scale * ffn_total).astype(jnp.bfloat16)
    merged = patch_out.reshape(SLOTS, 4, model_width)
    projected = jnp.zeros((SLOTS, DOUT), jnp.float32)
    for quarter in range(4):
        projected = projected + jnp.dot(merged[:, quarter, :], projection[quarter], preferred_element_type=jnp.float32)
    projected = projected.astype(jnp.bfloat16)
    target = jnp.where(destination >= 0, destination, NS * L).astype(jnp.int32)
    streams = text_rows.at[target].set(projected, mode='drop')
    return (patch_out, streams)
```

```python
import functools

import jax
import jax.numpy as jnp
from jax import lax
from jax.experimental import pallas as pl
from jax.experimental.pallas import tpu as pltpu
from jax.sharding import Mesh
from jax.sharding import PartitionSpec as P

NX, NZ, NY, NC = 4, 4, 4, 2
AXES = ("x", "z", "y", "c")
SLOT = 32
BF = jnp.bfloat16
F32 = jnp.float32


def torus_pairs(first, step):
    pairs = []
    for x in range(NX):
        for z in range(NZ):
            for y in range(NY):
                for c in range(NC):
                    along_x = (c == 0) == first
                    tx = (x + step) % NX if along_x else x
                    tz = z if along_x else (z + step) % NZ
                    pairs.append(
                        (
                            ((x * NZ + z) * NY + y) * NC + c,
                            ((tx * NZ + tz) * NY + y) * NC + c,
                        )
                    )
    return pairs


PAIRS = {(f, s): torus_pairs(f, s) for f in (True, False) for s in (1, -1)}


def hop(value, first, step):
    return lax.ppermute(value, AXES, PAIRS[(first, step)])


def shift(value, axis, step):
    size = {"x": NX, "z": NZ, "y": NY, "c": NC}[axis]
    return lax.ppermute(value, axis, [(i, (i + step) % size) for i in range(size)])


def together(*values):
    return lax.optimization_barrier(values)


def lines_kernel(plan, own, low, high, far_a, far_b, wait_for, *refs):
    sources, outs, sems = (own, low, high, far_a, far_b), refs[:-1], refs[-1]
    copies = []
    for i, (source, at, rows, col, cols, out, to) in enumerate(plan):
        copies.append(
            pltpu.make_async_copy(
                sources[source].at[pl.ds(at, rows), pl.ds(col, cols)],
                outs[out].at[pl.ds(to, rows)],
                sems.at[i],
            )
        )
    for copy in copies:
        copy.start()
    for copy in copies:
        copy.wait()


def lines_plan(units, width):
    kinds = ((0, 0, width), (1, 0, width), (2, 0, width))
    cut = 3 * units // 2
    plan = []
    for out, (kind, col, cols) in enumerate(kinds):
        for device in range(3):
            plan.append((device, kind * units, units, col, cols, out, device * units))
        first = kind * units
        at = first
        while at < first + units:
            in_low = at < cut
            end = min(first + units, cut) if in_low else first + units
            source, row = (3, at) if in_low else (4, at - cut)
            plan.append((source, row, end - at, col, cols, out, 3 * units + at - first))
            at = end
    return plan


def make_lines(blocks, wait_for):
    width = blocks[0].shape[1]
    units = blocks[0].shape[0] // 3
    plan = lines_plan(units, width)
    any_spec = pl.BlockSpec(memory_space=pltpu.HBM)
    return pl.pallas_call(
        functools.partial(lines_kernel, plan),
        out_shape=[
            jax.ShapeDtypeStruct((4 * units, width), BF)
        ]
        * 3,
        in_specs=[any_spec] * 6,
        out_specs=[pl.BlockSpec(memory_space=pltpu.VMEM)] * 3,
        scratch_shapes=[pltpu.SemaphoreType.DMA((len(plan),))],
        compiler_params=pltpu.CompilerParams(vmem_limit_bytes=56 << 20),
        cost_estimate=pl.CostEstimate(
            flops=0, bytes_accessed=48 * units * width, transcendentals=0
        ),
        name="lines",
    )(*blocks, wait_for)


def line_gather(value, first):
    half = value.shape[0] // 2
    low = hop(value, first, 1)
    high = hop(value, first, -1)
    far_a = hop(low[:half], first, 1)
    far_b = hop(high[half:], first, -1)
    return value, low, high, far_a, far_b


def prepare_kernel(width, order_ref, gate_ref, up_ref, down_ref, out_ref, sems):
    units = gate_ref.shape[0]
    count = gate_ref.shape[1] // (2 * width)
    copies = [
        pltpu.make_async_copy(gate_ref, out_ref.at[pl.ds(0, units)], sems.at[0]),
        pltpu.make_async_copy(up_ref, out_ref.at[pl.ds(units, units)], sems.at[1]),
    ]
    for i in range(count):
        at = pl.multiple_of(order_ref[i] * 2 * width, 2 * width)
        for h in range(2):
            copies.append(
                pltpu.make_async_copy(
                    down_ref.at[:, pl.ds(at + h * width, width)],
                    out_ref.at[pl.ds(2 * units, units), pl.ds((h * count + i) * width, width)],
                    sems.at[len(copies)],
                )
            )
    for copy in copies:
        copy.start()
    for copy in copies:
        copy.wait()


def prepare(order, gate, up, down, width):
    units, cols = gate.shape
    return pl.pallas_call(
        functools.partial(prepare_kernel, width),
        out_shape=jax.ShapeDtypeStruct((3 * units, cols), BF),
        in_specs=[pl.BlockSpec(memory_space=pltpu.SMEM)]
        + [pl.BlockSpec(memory_space=pltpu.HBM)] * 3,
        out_specs=pl.BlockSpec(memory_space=pltpu.VMEM),
        scratch_shapes=[pltpu.SemaphoreType.DMA((2 + cols // width,))],
        compiler_params=pltpu.CompilerParams(vmem_limit_bytes=56 << 20),
        cost_estimate=pl.CostEstimate(
            flops=0, bytes_accessed=12 * units * cols, transcendentals=0
        ),
        name="prepare",
    )(order, gate, up, down)


def gated_kernel(count, normed_ref, *refs):
    gates, ups = refs[:count], refs[count : 2 * count]
    out_ref, gate_sum, up_sum = refs[2 * count :]
    k = pl.program_id(0)
    rows, units = out_ref.shape
    wide = units // count
    chunk = rows // 4

    @pl.when(k == 0)
    def _():
        gate_sum[...] = jnp.zeros_like(gate_sum)
        up_sum[...] = jnp.zeros_like(up_sum)

    def step(i, carry):
        here = pl.ds(pl.multiple_of(i * chunk, chunk), chunk)
        left = normed_ref[here, :]
        for j in range(count):
            cols = slice(j * wide, (j + 1) * wide)
            gate_sum[here, cols] += dot_t(left, gates[j][...])
            up_sum[here, cols] += dot_t(left, ups[j][...])
        return carry

    lax.fori_loop(0, 4, step, 0)

    @pl.when(k == pl.num_programs(0) - 1)
    def _():
        small = rows // 20

        def finish(i, carry):
            here = pl.ds(pl.multiple_of(i * small, small), small)
            out_ref[here, :] = (jax.nn.silu(gate_sum[here, :]) * up_sum[here, :]).astype(BF)
            return carry

        lax.fori_loop(0, 20, finish, 0)


def gated(normed, gates, ups):
    rows, width = normed.shape
    units = sum(g.shape[0] for g in gates)
    depth = 1024
    return pl.pallas_call(
        functools.partial(gated_kernel, len(gates)),
        out_shape=jax.ShapeDtypeStruct((rows, units), BF),
        grid=(width // depth,),
        in_specs=[pl.BlockSpec((rows, depth), lambda k: (0, k))]
        + [pl.BlockSpec((b.shape[0], depth), lambda k: (0, k)) for b in (*gates, *ups)],
        out_specs=pl.BlockSpec((rows, units), lambda k: (0, 0)),
        scratch_shapes=[pltpu.VMEM((rows, units), F32)] * 2,
        compiler_params=pltpu.CompilerParams(vmem_limit_bytes=36 << 20),
        cost_estimate=pl.CostEstimate(
            flops=4 * rows * units * width,
            bytes_accessed=2 * (rows + 2 * units) * width,
            transcendentals=rows * units,
        ),
        name="gated",
    )(normed, *gates, *ups)


def layer_norm(values, norm_gain, norm_bias):
    row_mean = jnp.mean(values, axis=-1, keepdims=True)
    centred = values - row_mean
    variance = jnp.mean(centred * centred, axis=-1, keepdims=True)
    return centred * lax.rsqrt(variance + 1e-06) * norm_gain + norm_bias


def dot_t(a, b):
    return lax.dot_general(a, b, (((1,), (1,)), ((), ())), preferred_element_type=F32)


def dot(a, b):
    return jnp.dot(a, b, preferred_element_type=F32)


def down_kernel(count, near_ref, far_ref, *refs):
    blocks, out_ref, weights, hidden_ref = refs[:count], *refs[count:]

    @pl.when(pl.program_id(0) == 0)
    def _():
        near = near_ref.shape[1]
        hidden_ref[:, :near] = near_ref[...]
        hidden_ref[:, near:] = far_ref[...]

    at = 0
    for block in blocks:
        weights[at : at + block.shape[0], :] = block[...]
        at += block.shape[0]
    rows = out_ref.shape[0]
    chunk = rows // 2

    def step(i, carry):
        here = pl.ds(pl.multiple_of(i * chunk, chunk), chunk)
        out_ref[here, :] = dot(hidden_ref[here, :], weights[...]).astype(out_ref.dtype)
        return carry

    lax.fori_loop(0, 2, step, 0)


def down_matmul(hidden, blocks, quarter):
    rows = hidden[0].shape[0]
    depth = sum(h.shape[1] for h in hidden)
    tile = 512
    count = blocks[0].shape[1] // (4 * tile)
    skip = quarter * count
    return pl.pallas_call(
        functools.partial(down_kernel, len(blocks)),
        out_shape=jax.ShapeDtypeStruct((rows, count * tile), BF),
        grid=(count,),
        in_specs=[pl.BlockSpec(h.shape, lambda i: (0, 0)) for h in hidden]
        + [pl.BlockSpec((b.shape[0], tile), lambda i: (0, i + skip)) for b in blocks],
        out_specs=pl.BlockSpec((rows, tile), lambda i: (0, i)),
        scratch_shapes=[pltpu.VMEM((depth, tile), BF), pltpu.VMEM((rows, depth), BF)],
        compiler_params=pltpu.CompilerParams(vmem_limit_bytes=24 << 20),
        cost_estimate=pl.CostEstimate(
            flops=2 * rows * depth * count * tile,
            bytes_accessed=rows * depth * 2 + depth * count * tile * 2 + rows * count * tile * 2,
            transcendentals=0,
        ),
        name="down",
    )(*hidden, *blocks)


def finish_kernel(half, both_ref, prev_ref, next_ref, patch_ref, scale_ref, *refs):
    merged_ref, total = refs[-2], refs[-1]
    wide = both_ref.shape[1]
    ffn = both_ref[...].astype(F32) + prev_ref[...].astype(F32) + next_ref[...].astype(F32)
    value = patch_ref[...].astype(F32) + scale_ref[...] * ffn
    for t in range(wide // 128):
        total[t] = value[:, t * 128 : (t + 1) * 128]
    if half:
        out_ref = refs[1]
        out_ref[:, :wide] = refs[0][...]
        out_ref[:, wide:] = value.astype(BF)
    else:
        refs[0][...] = value.astype(BF)
    per = merged_ref.shape[0]
    for q in range(4):
        for t in range(wide // 128):
            at = q * wide + t * 128
            merged_ref[:, at : at + 128] = total[t, pl.ds(q, per, stride=4), :].astype(BF)


def finish(half, both, from_prev, from_next, patches, scale, first):
    rows = patches.shape[0]
    wide = from_prev.shape[1]

    def mine(i):
        return (0, half)

    def whole(i):
        return (0, 0)

    block = pl.BlockSpec((rows, wide), whole)
    out_wide = 2 * wide if half else wide
    return pl.pallas_call(
        functools.partial(finish_kernel, half),
        out_shape=[
            jax.ShapeDtypeStruct((rows, out_wide), BF),
            jax.ShapeDtypeStruct((rows // 4, 4 * wide), BF),
        ],
        grid=(1,),
        in_specs=[
            block,
            block,
            block,
            pl.BlockSpec((rows, wide), mine),
            pl.BlockSpec((1, wide), mine),
        ]
        + [block] * half,
        out_specs=[
            pl.BlockSpec((rows, out_wide), whole),
            pl.BlockSpec((rows // 4, 4 * wide), whole),
        ],
        scratch_shapes=[pltpu.VMEM((wide // 128, rows, 128), F32)],
        compiler_params=pltpu.CompilerParams(vmem_limit_bytes=16 << 20),
        cost_estimate=pl.CostEstimate(
            flops=4 * rows * wide, bytes_accessed=14 * rows * wide, transcendentals=0
        ),
        name="finish",
    )(both, from_prev, from_next, patches, scale, *([first] if half else []))


def project_kernel(count, pick_ref, *refs):
    blocks, weights = refs[:count], refs[count]
    out_ref, rows, sems = refs[count + 1 :]
    per, depth = blocks[0].shape
    copies = []
    for i, block in enumerate(blocks):
        h, b = divmod(i, count // 2)
        copies.append(
            pltpu.make_async_copy(
                block, rows.at[pl.ds(b * per, per), pl.ds(h * depth, depth)], sems.at[i]
            )
        )
    for copy in copies:
        copy.start()
    for copy in copies:
        copy.wait()
    total = rows.shape[0]
    chunk = total // 2
    wide = weights.shape[2]

    def step(i, carry):
        here = pl.ds(pl.multiple_of(i * chunk, chunk), chunk)
        for j in range(2):
            out_ref[here, j * wide : (j + 1) * wide] = dot(rows[here, :], weights[j]).astype(BF)
        return carry

    lax.fori_loop(0, 2, step, 0)


def project(blocks, weights, core):
    per, depth = blocks[0].shape
    total = per * len(blocks) // 2
    wide = weights.shape[2]
    pick = core.astype(jnp.int32)[None]
    return pl.pallas_call(
        functools.partial(project_kernel, len(blocks)),
        out_shape=jax.ShapeDtypeStruct((total, 2 * wide), BF),
        grid_spec=pltpu.PrefetchScalarGridSpec(
            num_scalar_prefetch=1,
            grid=(1,),
            in_specs=[pl.BlockSpec(memory_space=pl.ANY)] * len(blocks)
            + [pl.BlockSpec((2, 2 * depth, wide), lambda i, pick_ref: (pick_ref[0], 0, 0))],
            out_specs=pl.BlockSpec((total, 2 * wide), lambda i, pick_ref: (0, 0)),
            scratch_shapes=[
                pltpu.VMEM((total, 2 * depth), BF),
                pltpu.SemaphoreType.DMA((len(blocks),)),
            ],
        ),
        compiler_params=pltpu.CompilerParams(vmem_limit_bytes=24 << 20),
        cost_estimate=pl.CostEstimate(
            flops=8 * total * depth * wide,
            bytes_accessed=4 * total * (depth + wide) + 8 * depth * wide,
            transcendentals=0,
        ),
        name="project",
    )(pick, *blocks, weights)


def fill_kernel(in_ref, out_ref):
    out_ref[...] = in_ref[...]


def fill(value):
    rows, width = value.shape
    spec = pl.BlockSpec((rows // 8, width), lambda i: (i, 0))
    return pl.pallas_call(
        fill_kernel,
        out_shape=jax.ShapeDtypeStruct(value.shape, value.dtype),
        grid=(8,),
        in_specs=[spec],
        out_specs=spec,
        compiler_params=pltpu.CompilerParams(vmem_limit_bytes=8 << 20),
        cost_estimate=pl.CostEstimate(flops=0, bytes_accessed=4 * value.size, transcendentals=0),
        name="fill",
    )(value)


WINDOW = 48


def place_kernel(meta_ref, own_ref, other_ref, filled_ref, out_ref, window, sem):
    start, count, core, z = meta_ref[0], meta_ref[1], meta_ref[2], meta_ref[3]
    total_rows = filled_ref.shape[0]
    first = jnp.minimum((start // 16) * 16, total_rows - WINDOW)
    first = pl.multiple_of(first, 16)
    fetch = pltpu.make_async_copy(filled_ref.at[pl.ds(first, WINDOW)], window, sem.at[0])
    fetch.start()
    rank = lax.broadcasted_iota(jnp.int32, (WINDOW, SLOT), 0) + first - start
    slot = lax.broadcasted_iota(jnp.int32, (WINDOW, SLOT), 1)
    pick = ((rank == slot) & (slot < count)).astype(F32).astype(BF)
    width = window.shape[1] // 16
    row = lax.broadcasted_iota(jnp.int32, (WINDOW, width), 0) + first - start
    inside = (row >= 0) & (row < count)
    fetch.wait()

    for j in range(16):
        entry = lax.rem(j % 4 + NZ - z, NZ)
        half = (j // 4) % 2
        cols = pl.ds(half * width, width)
        image = jnp.where(core == j // 8, own_ref[entry, :, cols], other_ref[entry, :, cols])
        placed = dot(pick, image)
        at = pl.ds(j * width, width)
        window[:, at] = jnp.where(inside, placed, window[:, at].astype(F32)).astype(window.dtype)
    put = pltpu.make_async_copy(window, out_ref.at[pl.ds(first, WINDOW)], sem.at[1])
    put.start()
    put.wait()


def place_rows(meta, own, other, filled):
    return pl.pallas_call(
        place_kernel,
        out_shape=jax.ShapeDtypeStruct(filled.shape, filled.dtype),
        in_specs=[
            pl.BlockSpec(memory_space=pltpu.SMEM),
            pl.BlockSpec(memory_space=pltpu.VMEM),
            pl.BlockSpec(memory_space=pltpu.VMEM),
            pl.BlockSpec(memory_space=pl.ANY),
        ],
        out_specs=pl.BlockSpec(memory_space=pl.ANY),
        scratch_shapes=[
            pltpu.VMEM((WINDOW, filled.shape[1]), filled.dtype),
            pltpu.SemaphoreType.DMA((2,)),
        ],
        input_output_aliases={3: 0},
        cost_estimate=pl.CostEstimate(
            flops=2 * WINDOW * SLOT * filled.shape[1],
            bytes_accessed=4 * WINDOW * filled.shape[1],
            transcendentals=0,
        ),
        name="place",
    )(meta, own, other, filled)


def shards(
    patches,
    norm_gain,
    norm_bias,
    gate_weight,
    up_weight,
    down_weight,
    layer_scale,
    projection,
    text_rows,
    destination,
):
    x = lax.axis_index("x")
    z = lax.axis_index("z")
    y = lax.axis_index("y")
    c = lax.axis_index("c")
    rows_here, model_width = patches.shape
    owners = NY * NC
    feat_width = model_width // owners
    half_width = feat_width // 2
    merged_rows = rows_here // 4
    out_width = projection.shape[2]

    around = ((y + jnp.arange(NY, dtype=jnp.int32)) % NY) * NC
    owner_order = jnp.concatenate([around + 1 - c, around + c]).astype(jnp.int32)
    own = prepare(owner_order, gate_weight.T, up_weight.T, down_weight.T, half_width)
    parts = line_gather(own, True)
    inputs = patches.astype(F32)
    normed = layer_norm(inputs, norm_gain, norm_bias).astype(BF)
    gate_own, up_own, down_own = make_lines(parts, normed[:8, :128])
    gate_own, up_own, text_rows, destination = together(gate_own, up_own, text_rows, destination)

    piece_rows = text_rows.shape[0]
    pieces = NX * NZ * owners
    is_valid = destination >= 0
    piece_ids = jnp.where(is_valid, destination // piece_rows, -1)
    offsets = destination % piece_rows
    hit = piece_ids[:, None] == jnp.arange(pieces, dtype=jnp.int32)[None, :]
    first_off = jnp.min(jnp.where(hit, offsets[:, None], piece_rows), axis=0)
    counts = jnp.sum(hit.astype(jnp.int32), axis=0)
    slot_first = jnp.sum(jnp.where(hit, first_off[None, :], 0), axis=1)
    owner_ids = piece_ids % owners
    slots = ((piece_ids // owners) * NC + owner_ids % NC) * SLOT + offsets - slot_first
    slots = jnp.where(is_valid & (owner_ids // NC == y), slots, -1)
    ring = jnp.array([0, -1, 1, 2], jnp.int32)
    own_slots = []
    for t in (0, -1, 1, 2):
        source = (z + ring[(y + t) % NY]) % NZ
        own_slots.append(lax.dynamic_slice_in_dim(slots, (x * NZ + source) * merged_rows, merged_rows))
    own_slots = jnp.concatenate(own_slots)
    slot_count = NX * NZ * NC * SLOT
    select = (jnp.arange(slot_count, dtype=jnp.int32)[:, None] == own_slots[None, :]).astype(BF)

    here = (x * NZ + z) * owners + y * NC + c
    meta = jnp.stack([first_off[here], counts[here], c, z]).astype(jnp.int32)
    filled = fill(text_rows)
    owned = (y * NC + c) * feat_width
    scale_here = lax.dynamic_slice_in_dim(layer_scale, owned, feat_width)[None, :]
    own_patches = lax.dynamic_slice_in_dim(patches, owned, feat_width, axis=1)
    weight_own = projection.reshape(4, 2, half_width, out_width).transpose(1, 0, 2, 3)
    weight_own = weight_own.reshape(4 * feat_width, out_width)
    gate_low, up_high = hop(gate_own, False, 1), hop(up_own, False, -1)
    up_low, gate_high = hop(up_own, False, 1), hop(gate_own, False, -1)
    gate_low, up_high, up_low, gate_high, down_own, select, filled, meta = together(
        gate_low, up_high, up_low, gate_high, down_own, select, filled, meta
    )
    scale_here, own_patches, weight_own, down_own = together(
        scale_here, own_patches, weight_own, down_own
    )
    hidden_near = gated(normed, (gate_own, gate_low, gate_high), (up_own, up_low, up_high))
    gate_far, up_far = hop(gate_low, False, 1), hop(up_high, False, -1)
    down_low, down_high = hop(down_own, False, 1), hop(down_own, False, -1)
    gate_far, up_far, down_low, down_high, hidden_near = together(
        gate_far, up_far, down_low, down_high, hidden_near
    )
    cut = down_own.shape[0] // 2
    down_far_a, down_far_b = hop(down_low[:cut], False, 1), hop(down_high[cut:], False, -1)
    down_blocks = (down_own, down_low, down_high, down_far_a, down_far_b)
    hidden_far = gated(normed, (gate_far,), (up_far,))
    hidden = (hidden_near, hidden_far)

    weight_own, *hidden = together(weight_own, *hidden)
    columns = lax.all_gather(weight_own, "x", axis=0, tiled=True)
    columns = columns.reshape(NX, 4 * feat_width, out_width)

    patch_out, row_blocks = None, []
    for h in range(2):
        to_core = down_matmul(hidden, down_blocks, 2 * h)
        from_core = shift(to_core, "c", 1)
        kept = down_matmul(hidden, down_blocks, 2 * h + 1)
        both = [
            kept[:, d * half_width : (d + 1) * half_width].astype(F32)
            + from_core[:, d * half_width : (d + 1) * half_width].astype(F32)
            for d in range(NY)
        ]
        both_bf = [v.astype(BF) for v in both]
        cut = rows_here // 2
        up_part = shift(both_bf[2][:cut], "y", 1)
        low_part = shift(both_bf[2][cut:], "y", -1)
        to_next = jnp.concatenate(
            [(both[1][:cut] + up_part.astype(F32)).astype(BF), both_bf[1][cut:]], axis=0
        )
        to_prev = jnp.concatenate(
            [both_bf[3][:cut], (both[3][cut:] + low_part.astype(F32)).astype(BF)], axis=0
        )
        patch_out, merged = finish(
            h,
            both_bf[0],
            shift(to_next, "y", 1),
            shift(to_prev, "y", -1),
            own_patches,
            scale_here,
            patch_out,
        )
        if h == 1:
            merged, *row_blocks = together(merged, *row_blocks)
        row_blocks += [
            merged, shift(merged, "z", 1), shift(merged, "z", -1), shift(merged, "z", 2)
        ]
    theirs = project(row_blocks, columns, 1 - c)
    from_core = shift(theirs, "c", 1)
    mine = project(row_blocks, columns, c)

    total = mine.astype(F32) + from_core.astype(F32)

    def row_block(d):
        return lax.dynamic_slice_in_dim(total, ((y + d) % NY) * merged_rows, merged_rows)

    summed = row_block(0)
    for d in (1, 3, 2):
        summed = summed + shift(row_block(d).astype(BF), "y", d).astype(F32)
    summed = summed.astype(BF)
    everyone = jnp.concatenate(
        [summed, shift(summed, "y", 1), shift(summed, "y", -1), shift(summed, "y", 2)], axis=0
    )
    chosen = dot(select, everyone).astype(BF)
    per_x = NZ * NC * SLOT

    def x_block(d):
        return lax.dynamic_slice_in_dim(chosen, ((x + d) % NX) * per_x, per_x)

    arrived = x_block(0)
    for d in (1, 3, 2):
        arrived = arrived + shift(x_block(d), "x", d)
    per_z = NC * SLOT

    def z_block(d):
        return lax.dynamic_slice_in_dim(arrived, ((z + d) % NZ) * per_z, per_z)

    by_z = [z_block(0)] + [shift(z_block((-d) % NZ), "z", -d) for d in (1, 2, 3)]
    by_z = jnp.stack(by_z).reshape(NZ, NC, SLOT, -1)
    own = lax.dynamic_index_in_dim(by_z, c, 1, keepdims=False)
    other = shift(lax.dynamic_index_in_dim(by_z, 1 - c, 1, keepdims=False), "c", 1)
    streams = place_rows(meta, own, other, filled)
    return (patch_out, streams)


def solution(mesh):
    fine = Mesh(mesh.devices.reshape(NX, NZ, NY, NC), AXES)
    req, mlp = ("x", "z"), ("y", "c")
    both = req + mlp
    return jax.shard_map(
        shards,
        mesh=fine,
        in_specs=(
            P(req, None),
            P(),
            P(),
            P(None, both),
            P(None, both),
            P(None, both),
            P(),
            P(None, mlp, req),
            P(both, None),
            P(),
        ),
        out_specs=(P(req, mlp), P(both, None)),
        check_vma=False,
    )
```
